32 devices in a mesh: sx: 8 (over z, y), sy: 4 (over x, core).
Axes of the slice: x: 2, y: 2, z: 4, core: 2. Of those that a mesh axis runs over, the one named last changes fastest.
Arguments:
- schur: bfloat16 [8, 4096, 4096], P('sx', 'sy'), as said below
- precond: bfloat16 [8, 4096, 4096], P('sx', 'sy'), as said below
- right_side: float32 [8, 32, 2048], P('sx', None, 'sy')
- matching: int32 [8, 2048], P('sx', 'sy'), may hold values from 0 to 511, as said below
Outputs:
- solution: float32 [8, 32, 2048], P('sx', None, 'sy')
- residual: float32 [8, 32, 2048], P('sx', None, 'sy')
The draws below stay inside these ranges and needn't reach their ends.
Inputs may be any that keep to these rules, and one draw needn't show every extreme that they name: `schur`: each subdomain's matrix is symmetric positive definite. `precond`: each subdomain's matrix is symmetric positive definite. `matching`: each aligned block of 512 entries of a row is a permutation of 0 to 511.
All inputs are finite; a program needn't handle non-finite values.
Results may differ from the reference program's by a relative error of at most 0.007.
The reference program's roundings to bfloat16 on the way count: a program that leaves them out, or rounds other values in their place, can miss the bound.
Values may be sent and summed in bfloat16 or wider, within the bound.
No kernel may reach another device: no remote copies, remote signals or barrier semaphores. Data moves between devices by JAX's collectives and lax.ppermute only.
A program may use at most 64 MiB of HBM per device.

```python
import math
import jax
import jax.numpy as jnp
from jax import lax

NLOC = 4096
K = 32
ITERS = 2
NSUB = 8
FACE = 2048
FB = 512


def spd_blocks(key, low, high, factor):
    keys = jax.random.split(jax.random.fold_in(key, 11), NSUB)
    dkey = jax.random.fold_in(key, 23)
    diag_rows = low * jnp.exp(math.log(high / low) * jax.random.uniform(dkey, (NSUB, NLOC), jnp.float32))
    rows = lax.broadcasted_iota(jnp.int32, (NLOC, NLOC), 0)
    cols = lax.broadcasted_iota(jnp.int32, (NLOC, NLOC), 1)

    def one(pair):
        sub_key, diag_one = pair
        entries = jnp.clip(jax.random.normal(sub_key, (NLOC, NLOC), jnp.float32), -3.0, 3.0)
        coupled = (entries + entries.T) * (factor / math.sqrt(NLOC))
        return jnp.where(rows == cols, diag_one[:, None], coupled).astype(jnp.bfloat16)
    return lax.map(one, (keys, diag_rows))


def draw_schur(key, part):
    return spd_blocks(jax.random.fold_in(key, 101), 1.0, 2.0, 0.25)


def draw_precond(key, part):
    return spd_blocks(jax.random.fold_in(key, 202), 0.6, 1.2, 0.12)


def draw_right_side(key, part):
    sub = lax.broadcasted_iota(jnp.float32, (NSUB, 1, 1), 0) / max(NSUB - 1, 1)
    pos = lax.broadcasted_iota(jnp.float32, (1, 1, FACE), 2) / max(FACE - 1, 1)
    ramp = jnp.power(3.0, sub) * jnp.power(3.0, pos)
    k1 = jax.random.fold_in(jax.random.fold_in(key, 303), 0)
    return jax.random.normal(k1, (NSUB, K, FACE), jnp.float32) * ramp


def draw_matching(key, part):
    keys = jax.random.split(jax.random.fold_in(key, 404), NSUB * (FACE // FB))
    perms = jax.vmap(lambda one_key: jax.random.permutation(one_key, FB))(keys)
    return perms.reshape(NSUB, FACE).astype(jnp.int32)


def setup_inputs(seed: int = 0) -> dict:
    key_of = jax.random.split(jax.random.key(seed), 5)
    schur = draw_schur(jax.random.fold_in(key_of[4], 71), 0)
    precond = draw_precond(jax.random.fold_in(key_of[4], 71), 0)
    right_side = draw_right_side(jax.random.fold_in(key_of[4], 71), 0)
    matching = draw_matching(jax.random.fold_in(key_of[4], 71), 0)
    return {"schur": schur, "precond": precond, "right_side": right_side, "matching": matching}


def face_maps(matching):
    offsets = lax.broadcasted_iota(jnp.int32, matching.shape, 1) // FB * FB
    gidx = (matching + offsets).astype(jnp.int32)
    inverse = jnp.argsort(gidx, axis=1).astype(jnp.int32)
    return (gidx, inverse)

def apply_op(matrix, block, gidx, inverse):
    taken = jnp.take_along_axis(block, gidx[:, None, :], axis=2)
    right_part = jnp.roll(taken, -1, axis=0)
    nblocks = FACE // FB
    left_view = block.reshape(NSUB, K, nblocks, FB)
    right_view = right_part.reshape(NSUB, K, nblocks, FB)
    local = jnp.concatenate([left_view, right_view], axis=3).reshape(NSUB, K, NLOC)

    def one(pair):
        mat, vec = pair
        return jnp.dot(vec.astype(jnp.float32), mat.T.astype(jnp.float32), preferred_element_type=jnp.float32)
    prod = lax.map(one, (matrix, local)).reshape(NSUB, K, nblocks, 2 * FB)
    left_out = prod[:, :, :, :FB].reshape(NSUB, K, FACE)
    right_out = prod[:, :, :, FB:].reshape(NSUB, K, FACE)
    came = jnp.roll(right_out, 1, axis=0)
    return left_out + jnp.take_along_axis(came, inverse[:, None, :], axis=2)

def gram(first, second):
    total = jnp.einsum('jkf,jlf->kl', first, second, precision=lax.Precision.HIGHEST)
    return 0.5 * (total + total.T)

def solve_spd(matrix, rhs):
    lower = jnp.linalg.cholesky(matrix)
    return jax.scipy.linalg.cho_solve((lower, True), rhs)

def combine(coeff, block):
    return jnp.einsum('kl,jkf->jlf', coeff, block, precision=lax.Precision.HIGHEST)

def reference(schur, precond, right_side, matching):
    gidx, inverse = face_maps(matching)
    residual = right_side
    solution = jnp.zeros_like(right_side)
    search = apply_op(precond, residual.astype(jnp.bfloat16), gidx, inverse)
    gamma = gram(residual, search)
    for step in range(ITERS):
        image = apply_op(schur, search.astype(jnp.bfloat16), gidx, inverse)
        delta = gram(search, image)
        alpha = solve_spd(delta, gamma)
        solution = solution + combine(alpha, search)
        residual = residual - combine(alpha, image)
        if step + 1 < ITERS:
            precd = apply_op(precond, residual.astype(jnp.bfloat16), gidx, inverse)
            gnew = gram(residual, precd)
            beta = solve_spd(gamma, gnew)
            search = precd + combine(beta, search)
            gamma = gnew
    return (solution, residual)
```

```python
import functools

import jax
import jax.numpy as jnp
from jax import lax
from jax.experimental import pallas as pl
from jax.experimental.pallas import tpu as pltpu
from jax.sharding import PartitionSpec as P


LANES = 128
AXES = ("sx", "sy")
HIGH = lax.Precision.HIGHEST
VMEM = pl.BlockSpec(memory_space=pltpu.VMEM)


def call(body, outs, *args, flops=1 << 20, touched=1 << 20):
    return pl.pallas_call(
        body,
        out_shape=outs,
        in_specs=[VMEM] * len(args),
        out_specs=jax.tree.map(lambda _: VMEM, outs),
        cost_estimate=pl.CostEstimate(flops=flops, bytes_accessed=touched, transcendentals=0),
    )(*args)


def f32(*shape):
    return jax.ShapeDtypeStruct(shape, jnp.float32)


def bf16(*shape):
    return jax.ShapeDtypeStruct(shape, jnp.bfloat16)


def passed_along(block, distance):
    devices = range(lax.axis_size("sx"))
    route = [((i - distance) % len(devices), i) for i in devices]
    return lax.ppermute(block, "sx", route)


def select(value, onehot, axis):
    k = value.shape[0]
    high = value.astype(jnp.bfloat16)
    rest = value - high.astype(jnp.float32)
    mid = rest.astype(jnp.bfloat16)
    low = (rest - mid.astype(jnp.float32)).astype(jnp.bfloat16)
    pieces = jnp.concatenate([high, mid, low], axis=0)
    picked = lax.dot_general(pieces, onehot, (((1,), (axis,)), ((), ())), preferred_element_type=jnp.float32)
    return (picked[:k] + picked[k : 2 * k]) + picked[2 * k :]


def gram(first, second):
    return lax.dot_general(first, second, (((1,), (1,)), ((), ())), precision=HIGH, preferred_element_type=jnp.float32)


def combine(coeff, block):
    return lax.dot_general(coeff, block, (((0,), (0,)), ((), ())), precision=HIGH, preferred_element_type=jnp.float32)


def pack(square):
    k = square.shape[0]
    pieces = LANES // k
    rows = k // pieces
    return jnp.concatenate([square[i * rows : (i + 1) * rows] for i in range(pieces)], axis=1)


def unpack(tile, k):
    pieces = LANES // k
    square = jnp.concatenate([tile[:, i * k : (i + 1) * k] for i in range(pieces)], axis=0)
    return 0.5 * (square + square.T)


def eliminate(table, k, systems):
    lane = lax.broadcasted_iota(jnp.int32, table.shape, 1)
    line = lax.broadcasted_iota(jnp.int32, table.shape, 0)
    for step in range(k):
        column = jnp.broadcast_to(table[:, step : step + 1], table.shape)
        for s in range(1, systems):
            other = jnp.broadcast_to(table[:, 2 * k * s + step : 2 * k * s + step + 1], table.shape)
            column = jnp.where(lane < 2 * k * s, column, other)
        scaled = table[step : step + 1] / column[step : step + 1]
        table = jnp.where(line == step, scaled, table - column * scaled)
    return table


def send_kernel(value, onehot, out):
    out[...] = select(value[...], onehot[...], 1)


def apply_kernel(with_select, gathered, matrix, weights, onehot, product, *chosen):
    rows = matrix.shape[0]
    half = rows // 2
    step = min(256, half)
    for n in range(0, rows, step):
        product[:, n : n + step] = lax.dot_general(
            gathered[...], matrix[n : n + step, :], (((1,), (1,)), ((), ())), preferred_element_type=jnp.float32
        )
    if with_select:
        chosen[0][...] = select(product[:, :half], onehot[...], 1)


def gram_kernel(pairs, *refs):
    out = refs[-1]
    tiles = [pack(gram(refs[2 * i][...], refs[2 * i + 1][...])) for i in range(pairs)]
    tile = jnp.concatenate(tiles, axis=0)
    out[...] = jnp.broadcast_to(tile[None], out.shape)


def assembled(product, from_left, from_right, onehot):
    half = product.shape[1] // 2
    left = product[:, :half] + select(from_left[...], onehot[...], 0)
    right = product[:, half:] + from_right[...]
    return jnp.concatenate([left, right], axis=1)


def direction_kernel(product, from_left, from_right, onehot, search, rounded):
    search[...] = assembled(product, from_left, from_right, onehot)
    rounded[...] = search[...].astype(jnp.bfloat16)


def alpha_kernel(partials, product, from_left, from_right, onehot, residual, new_residual, rounded, solved):
    k = residual.shape[0]
    total = jnp.sum(partials[...], axis=0)
    half = total.shape[0] // 2
    gamma = unpack(total[:half], k)
    delta = unpack(total[half:], k)
    line = lax.broadcasted_iota(jnp.int32, (k, k), 0)
    lane = lax.broadcasted_iota(jnp.int32, (k, k), 1)
    eye = jnp.where(line == lane, 1.0, 0.0).astype(jnp.float32)
    table = eliminate(jnp.concatenate([delta, gamma, gamma, eye], axis=1), k, 2)
    solved[...] = table
    image = assembled(product, from_left, from_right, onehot)
    new_residual[...] = residual[...] - combine(table[:, k : 2 * k], image)
    rounded[...] = new_residual[...].astype(jnp.bfloat16)


def beta_kernel(partials, product, from_left, from_right, onehot, search, solved, new_search, rounded, gnew):
    k = search.shape[0]
    fresh = unpack(jnp.sum(partials[...], axis=0), k)
    gnew[...] = fresh
    beta = lax.dot_general(
        solved[:, 3 * k : 4 * k], fresh, (((1,), (0,)), ((), ())), precision=HIGH, preferred_element_type=jnp.float32
    )
    new_search[...] = assembled(product, from_left, from_right, onehot) + combine(beta, search[...])
    rounded[...] = new_search[...].astype(jnp.bfloat16)


def last_kernel(partials, product, from_left, onehot, residual, search, new_search, solved, gnew, sol, res):
    k = residual.shape[0]
    half = product.shape[1] // 2
    delta = unpack(jnp.sum(partials[...], axis=0), k)
    pad = jnp.zeros((k, LANES - 2 * k), jnp.float32)
    table = eliminate(jnp.concatenate([delta, gnew[...], pad], axis=1), k, 1)
    alpha = table[:, k : 2 * k]
    left = product[:, :half] + select(from_left[...], onehot[...], 0)
    res[...] = residual[:, :half] - combine(alpha, left)
    sol[...] = combine(solved[:, k : 2 * k], search[:, :half]) + combine(alpha, new_search[:, :half])


def spread(partials):
    return lax.all_to_all(partials, AXES, 0, 0)


def shards(schur, precond, right_side, matching):
    schur_rows = schur[0]
    precond_rows = precond[0]
    match_loc = matching[0]
    start = right_side[0]
    k, face = start.shape
    count = lax.axis_size("sx") * lax.axis_size("sy")
    tile_rows = k * k // LANES
    onehot = (match_loc[:, None] == lax.broadcasted_iota(jnp.int32, (face, face), 1)).astype(jnp.bfloat16)

    def apply(rounded, matrix, weights, with_select=True):
        gathered = lax.all_gather(rounded, "sy", axis=1, tiled=True)
        outs = (f32(k, 2 * face),) + ((f32(k, face),) if with_select else ())
        made = call(
            functools.partial(apply_kernel, with_select), outs, gathered, matrix, weights, onehot,
            flops=2 * k * matrix.size, touched=2 * matrix.size,
        )
        from_left = passed_along(made[0][:, face:], 1)
        from_right = passed_along(made[1], -1) if with_select else None
        return made[0], from_left, from_right

    def reduced(*pairs):
        out = f32(count, len(pairs) * tile_rows, LANES)
        flat = [v for pair in pairs for v in pair]
        return spread(call(functools.partial(gram_kernel, len(pairs)), out, *flat))

    right = passed_along(call(send_kernel, f32(k, face), start, onehot), -1)
    residual = jnp.concatenate([start, right], axis=1)
    product0, left0, right0 = apply(residual.astype(jnp.bfloat16), precond_rows, residual)
    search, rounded = call(direction_kernel, (f32(k, 2 * face), bf16(k, 2 * face)), product0, left0, right0, onehot)

    product, from_left, from_right = apply(rounded, schur_rows, search)
    partials = reduced((residual, product0), (search, product))
    residual, rounded, solved = call(
        alpha_kernel, (f32(k, 2 * face), bf16(k, 2 * face), f32(k, LANES)),
        partials, product, from_left, from_right, onehot, residual,
    )

    product, from_left, from_right = apply(rounded, precond_rows, residual)
    partials = reduced((residual, product))
    new_search, rounded, gnew = call(
        beta_kernel, (f32(k, 2 * face), bf16(k, 2 * face), f32(k, k)),
        partials, product, from_left, from_right, onehot, search, solved,
    )

    product, from_left, _ = apply(rounded, schur_rows, new_search, with_select=False)
    partials = reduced((new_search, product))
    sol, res = call(
        last_kernel, (f32(k, face), f32(k, face)),
        partials, product, from_left, onehot, residual, search, new_search, solved, gnew,
    )
    return (sol[None], res[None])


def solution(mesh):
    in_specs = (P("sx", "sy", None), P("sx", "sy", None), P("sx", None, "sy"), P("sx", "sy"))
    out_specs = (P("sx", None, "sy"), P("sx", None, "sy"))
    return jax.shard_map(shards, mesh=mesh, in_specs=in_specs, out_specs=out_specs, check_vma=False)
```

```python
import functools

import jax
import jax.numpy as jnp
from jax import lax
from jax.experimental import pallas as pl
from jax.experimental.pallas import tpu as pltpu
from jax.sharding import PartitionSpec as P


LANES = 128
BUDGET = 55 << 20
AXES = ("sx", "sy")
HIGH = lax.Precision.HIGHEST
VMEM = pl.BlockSpec(memory_space=pltpu.VMEM)


def call(body, outs, *args, places=None, scratch=(), room=0):
    room = room or (4 << 20) + sum(2 * a.size * a.dtype.itemsize for a in args if a.ndim == 3)
    return pl.pallas_call(
        body,
        out_shape=outs,
        in_specs=places or [VMEM] * len(args),
        out_specs=jax.tree.map(lambda _: VMEM, outs),
        scratch_shapes=scratch,
        cost_estimate=pl.CostEstimate(flops=1 << 24, bytes_accessed=1 << 23, transcendentals=0),
        compiler_params=pltpu.CompilerParams(vmem_limit_bytes=room),
    )(*args)


def f32(*shape):
    return jax.ShapeDtypeStruct(shape, jnp.float32)


def bf16(*shape):
    return jax.ShapeDtypeStruct(shape, jnp.bfloat16)


def passed_along(block, distance):
    devices = range(lax.axis_size("sx"))
    route = [((i - distance) % len(devices), i) for i in devices]
    return lax.ppermute(block, "sx", route)


def swapped(block, first):
    n = lax.axis_size("sx")
    route = []
    for i in range(first, n, 2):
        j = (i + 1) % n
        route += [(i, j), (j, i)]
    return lax.ppermute(block, "sx", route)


def partner(block, distance):
    return lax.ppermute(block, "sy", [(i, i ^ distance) for i in range(lax.axis_size("sy"))])


def select(value, chosen, axis):
    k = value.shape[0]
    high = value.astype(jnp.bfloat16)
    rest = value - high.astype(jnp.float32)
    mid = rest.astype(jnp.bfloat16)
    low = (rest - mid.astype(jnp.float32)).astype(jnp.bfloat16)
    pieces = jnp.concatenate([high, mid, low], axis=0)
    picked = lax.dot_general(pieces, chosen, (((1,), (axis,)), ((), ())), preferred_element_type=jnp.float32)
    return (picked[:k] + picked[k : 2 * k]) + picked[2 * k :]


def gram(first, second):
    return lax.dot_general(first, second, (((1,), (1,)), ((), ())), precision=HIGH, preferred_element_type=jnp.float32)


def combine(coeff, block):
    return lax.dot_general(coeff, block, (((0,), (0,)), ((), ())), precision=HIGH, preferred_element_type=jnp.float32)


def pack(square):
    k = square.shape[0]
    pieces = LANES // k
    rows = k // pieces
    return jnp.concatenate([square[i * rows : (i + 1) * rows] for i in range(pieces)], axis=1)


def unpack(tile, k):
    pieces = LANES // k
    square = jnp.concatenate([tile[:, i * k : (i + 1) * k] for i in range(pieces)], axis=0)
    return 0.5 * (square + square.T)


def eliminate(table, k, systems):
    lane = lax.broadcasted_iota(jnp.int32, table.shape, 1)
    line = lax.broadcasted_iota(jnp.int32, table.shape, 0)

    def column(step):
        found = jnp.broadcast_to(table[:, step : step + 1], table.shape)
        for s in range(1, systems):
            at = 2 * k * s + step
            found = jnp.where(lane < 2 * k * s, found, jnp.broadcast_to(table[:, at : at + 1], table.shape))
        return found

    for step in range(0, k, 2):
        one, two = column(step), column(step + 1)
        row_one, row_two = table[step : step + 1], table[step + 1 : step + 2]
        a, b = one[step : step + 1], two[step : step + 1]
        c, d = one[step + 1 : step + 2], two[step + 1 : step + 2]
        scale = 1.0 / (a * d - b * c)
        new_one = (d * row_one - b * row_two) * scale
        new_two = (a * row_two - c * row_one) * scale
        table = table - one * new_one - two * new_two
        table = jnp.where(line == step, new_one, jnp.where(line == step + 1, new_two, table))
    return table


def odd():
    return lax.rem(lax.axis_index("sx"), 2) == 1


def start_kernel(value, match, chosen, sent):
    face = value.shape[1]
    want = lax.broadcasted_iota(jnp.int32, (face, face), 0)
    chosen[...] = jnp.where(want == jnp.broadcast_to(match[...], (face, face)), 1.0, 0.0).astype(jnp.bfloat16)
    sent[...] = select(value[...], chosen[...], 0)


def near_kernel(size, own, beside, matrix, part, rest, held, sems):
    me = lax.axis_index("sy")
    rows, width = matrix.shape[0], own.shape[1]
    step = min(256, rows)
    copies = []
    for d in range(size):
        columns = pl.ds(pl.multiple_of((me ^ d) * width, width), width)
        target = held.at[d] if d < 2 else rest.at[d - 2]
        copies.append(pltpu.make_async_copy(matrix.at[:, columns], target, sems.at[d]))
        copies[-1].start()
    for d, block in enumerate((own, beside)):
        copies[d].wait()
        for n in range(0, rows, step):
            made = lax.dot_general(
                block[...], held[d, n : n + step, :], (((1,), (1,)), ((), ())), preferred_element_type=jnp.float32
            )
            part[:, n : n + step] = made if d == 0 else part[:, n : n + step] + made
    for d in range(2, size):
        copies[d].wait()


def far_kernel(far, mode, *refs):
    blocks = refs[:far]
    rest, part, weights, chosen = refs[far : far + 4]
    rows = part.shape[1]
    half = rows // 2
    step = min(256, half)
    if mode == "first":
        product, swap_even, swap_odd, tile = refs[far + 4 :]
    elif mode == "both":
        earlier, product, swap_even, swap_odd, out = refs[far + 4 :]
    elif mode == "one":
        product, swap_even, swap_odd, out = refs[far + 4 :]
    else:
        product, passed, out = refs[far + 4 :]
    for n in range(0, rows, step):
        made = part[:, n : n + step]
        for d in range(far):
            made = made + lax.dot_general(
                blocks[d][...], rest[d, n : n + step, :], (((1,), (1,)), ((), ())), preferred_element_type=jnp.float32
            )
        product[:, n : n + step] = made
    if mode == "last":
        passed[...] = product[:, half:]
    else:
        picked = select(product[:, :half], chosen[...], 0)
        right = product[:, half:]
        swap_even[...] = jnp.where(odd(), picked, right)
        swap_odd[...] = jnp.where(odd(), right, picked)
    fresh = pack(gram(weights[...], product[...]))
    if mode == "first":
        tile[...] = fresh
    else:
        if mode == "both":
            fresh = jnp.concatenate([earlier[...], fresh], axis=0)
        out[...] = jnp.broadcast_to(fresh[None], out.shape)


def assembled(product, got_even, got_odd, chosen):
    half = product.shape[1] // 2
    from_left = jnp.where(odd(), got_even[...], got_odd[...])
    from_right = jnp.where(odd(), got_odd[...], got_even[...])
    left = product[:, :half] + select(from_left, chosen[...], 1)
    return jnp.concatenate([left, product[:, half:] + from_right], axis=1)


def direction_kernel(product, got_even, got_odd, chosen, search, rounded):
    search[...] = assembled(product, got_even, got_odd, chosen)
    rounded[...] = search[...].astype(jnp.bfloat16)


def alpha_kernel(partials, product, got_even, got_odd, chosen, residual, new_residual, rounded, solved):
    k = residual.shape[0]
    total = jnp.sum(partials[...], axis=0)
    half = total.shape[0] // 2
    gamma = unpack(total[:half], k)
    delta = unpack(total[half:], k)
    line = lax.broadcasted_iota(jnp.int32, (k, k), 0)
    lane = lax.broadcasted_iota(jnp.int32, (k, k), 1)
    eye = jnp.where(line == lane, 1.0, 0.0).astype(jnp.float32)
    table = eliminate(jnp.concatenate([delta, gamma, gamma, eye], axis=1), k, 2)
    solved[...] = table
    image = assembled(product, got_even, got_odd, chosen)
    new_residual[...] = residual[...] - combine(table[:, k : 2 * k], image)
    rounded[...] = new_residual[...].astype(jnp.bfloat16)


def beta_kernel(partials, product, got_even, got_odd, chosen, search, solved, new_search, rounded, gnew):
    k = search.shape[0]
    fresh = unpack(jnp.sum(partials[...], axis=0), k)
    gnew[...] = fresh
    beta = lax.dot_general(
        solved[:, 3 * k : 4 * k], fresh, (((1,), (0,)), ((), ())), precision=HIGH, preferred_element_type=jnp.float32
    )
    new_search[...] = assembled(product, got_even, got_odd, chosen) + combine(beta, search[...])
    rounded[...] = new_search[...].astype(jnp.bfloat16)


def last_kernel(partials, product, from_left, chosen, residual, search, new_search, solved, gnew, sol, res):
    k = residual.shape[0]
    half = product.shape[1] // 2
    delta = unpack(jnp.sum(partials[...], axis=0), k)
    pad = jnp.zeros((k, LANES - 2 * k), jnp.float32)
    table = eliminate(jnp.concatenate([delta, gnew[...], pad], axis=1), k, 1)
    alpha = table[:, k : 2 * k]
    left = product[:, :half] + select(from_left[...], chosen[...], 1)
    res[...] = residual[:, :half] - combine(alpha, left)
    sol[...] = combine(solved[:, k : 2 * k], search[:, :half]) + combine(alpha, new_search[:, :half])


def spread(partials):
    return lax.all_to_all(partials, AXES, 0, 0)


def shards(schur, precond, right_side, matching):
    schur_rows = schur[0]
    precond_rows = precond[0]
    start = right_side[0]
    k, face = start.shape
    size = lax.axis_size("sy")
    count = lax.axis_size("sx") * size
    tile_rows = k * k // LANES
    chosen, sent = call(start_kernel, (bf16(face, face), f32(k, face)), start, matching)

    def apply(rounded, matrix, weights, mode, *earlier):
        far = [partner(rounded, d) for d in range(2, size)]
        beside = partner(rounded, 1)
        rows, width = matrix.shape[0], rounded.shape[1]
        room = 2 * matrix.size + (4 << 20)
        part, rest = call(
            functools.partial(near_kernel, size), (f32(k, rows), bf16(size - 2, rows, width)), rounded, beside, matrix,
            places=[VMEM, VMEM, pl.BlockSpec(memory_space=pltpu.HBM)],
            scratch=(pltpu.VMEM((2, rows, width), jnp.bfloat16), pltpu.SemaphoreType.DMA((size,))),
            room=BUDGET - matrix.size * 7 // 4,
        )
        swap = (f32(k, face), f32(k, face))
        outs = {
            "first": (f32(k, rows), *swap, f32(tile_rows, LANES)),
            "both": (f32(k, rows), *swap, f32(count, 2 * tile_rows, LANES)),
            "one": (f32(k, rows), *swap, f32(count, tile_rows, LANES)),
            "last": (f32(k, rows), f32(k, face), f32(count, tile_rows, LANES)),
        }[mode]
        return call(
            functools.partial(far_kernel, len(far), mode), outs, *far, rest, part, weights, chosen, *earlier, room=room
        )

    vectors = (f32(k, 2 * face), bf16(k, 2 * face))
    right = passed_along(sent, -1)
    residual = jnp.concatenate([start, right], axis=1)
    product, even, odd_, tile = apply(residual.astype(jnp.bfloat16), precond_rows, residual, "first")
    got_odd, got_even = swapped(odd_, 1), swapped(even, 0)
    search, rounded = call(direction_kernel, vectors, product, got_even, got_odd, chosen)

    product, even, odd_, partials = apply(rounded, schur_rows, search, "both", tile)
    partials = spread(partials)
    got_odd, got_even = swapped(odd_, 1), swapped(even, 0)
    residual, rounded, solved = call(
        alpha_kernel, (*vectors, f32(k, LANES)), partials, product, got_even, got_odd, chosen, residual
    )

    product, even, odd_, partials = apply(rounded, precond_rows, residual, "one")
    partials = spread(partials)
    got_odd, got_even = swapped(odd_, 1), swapped(even, 0)
    new_search, rounded, gnew = call(
        beta_kernel, (*vectors, f32(k, k)), partials, product, got_even, got_odd, chosen, search, solved
    )

    product, passed, partials = apply(rounded, schur_rows, new_search, "last")
    partials = spread(partials)
    from_left = passed_along(passed, 1)
    sol, res = call(
        last_kernel, (f32(k, face), f32(k, face)),
        partials, product, from_left, chosen, residual, search, new_search, solved, gnew,
    )
    return (sol[None], res[None])


def solution(mesh):
    in_specs = (P("sx", "sy", None), P("sx", "sy", None), P("sx", None, "sy"), P("sx", "sy"))
    out_specs = (P("sx", None, "sy"), P("sx", None, "sy"))
    return jax.shard_map(shards, mesh=mesh, in_specs=in_specs, out_specs=out_specs, check_vma=False)
```

```python
import functools

import jax
import jax.numpy as jnp
from jax import lax
from jax.experimental import pallas as pl
from jax.experimental.pallas import tpu as pltpu
from jax.sharding import PartitionSpec as P


LANES = 128
BUDGET = 55 << 20
AXES = ("sx", "sy")
HIGH = lax.Precision.HIGHEST
VMEM = pl.BlockSpec(memory_space=pltpu.VMEM)


def call(body, outs, *args, places=None, scratch=(), room=0):
    room = room or (4 << 20) + sum(2 * a.size * a.dtype.itemsize for a in args if a.ndim == 3)
    return pl.pallas_call(
        body,
        out_shape=outs,
        in_specs=places or [VMEM] * len(args),
        out_specs=jax.tree.map(lambda _: VMEM, outs),
        scratch_shapes=scratch,
        cost_estimate=pl.CostEstimate(flops=1 << 24, bytes_accessed=1 << 23, transcendentals=0),
        compiler_params=pltpu.CompilerParams(vmem_limit_bytes=room),
    )(*args)


def f32(*shape):
    return jax.ShapeDtypeStruct(shape, jnp.float32)


def bf16(*shape):
    return jax.ShapeDtypeStruct(shape, jnp.bfloat16)


def passed_along(block, distance):
    devices = range(lax.axis_size("sx"))
    route = [((i - distance) % len(devices), i) for i in devices]
    return lax.ppermute(block, "sx", route)


def swapped(block, first):
    n = lax.axis_size("sx")
    route = []
    for i in range(first, n, 2):
        j = (i + 1) % n
        route += [(i, j), (j, i)]
    return lax.ppermute(block, "sx", route)


def partner(block, distance):
    return lax.ppermute(block, "sy", [(i, i ^ distance) for i in range(lax.axis_size("sy"))])


def select(value, chosen, axis):
    k = value.shape[0]
    high = value.astype(jnp.bfloat16)
    rest = value - high.astype(jnp.float32)
    mid = rest.astype(jnp.bfloat16)
    low = (rest - mid.astype(jnp.float32)).astype(jnp.bfloat16)
    pieces = jnp.concatenate([high, mid, low], axis=0)
    picked = lax.dot_general(pieces, chosen, (((1,), (axis,)), ((), ())), preferred_element_type=jnp.float32)
    return (picked[:k] + picked[k : 2 * k]) + picked[2 * k :]


def gram(first, second):
    return lax.dot_general(first, second, (((1,), (1,)), ((), ())), precision=HIGH, preferred_element_type=jnp.float32)


def combine(coeff, block):
    return lax.dot_general(coeff, block, (((0,), (0,)), ((), ())), precision=HIGH, preferred_element_type=jnp.float32)


def pack(square):
    k = square.shape[0]
    pieces = LANES // k
    rows = k // pieces
    return jnp.concatenate([square[i * rows : (i + 1) * rows] for i in range(pieces)], axis=1)


def unpack(tile, k):
    pieces = LANES // k
    return jnp.concatenate([tile[:, i * k : (i + 1) * k] for i in range(pieces)], axis=0)


def halved(square):
    return 0.5 * (square + square.T)


def places(k):
    return lax.broadcasted_iota(jnp.int32, (k, k), 0), lax.broadcasted_iota(jnp.int32, (k, k), 1)


def pack_two(upper, lower):
    k = upper.shape[0]
    line, lane = places(k)
    tile = pack(jnp.where(line <= lane, upper, lower))
    diagonal = jnp.sum(jnp.where(line == lane, lower, 0.0), axis=0, keepdims=True)
    pad = jnp.zeros((1, LANES - k), jnp.float32)
    return [tile[i : i + 1] for i in range(tile.shape[0])] + [jnp.concatenate([diagonal, pad], axis=1)]


def unpack_two(row, k):
    line, lane = places(k)
    pieces = [row[:, i : i + LANES] for i in range(0, row.shape[1], LANES)]
    square = unpack(jnp.concatenate(pieces[:-1], axis=0), k)
    turned = square.T
    upper = jnp.where(line <= lane, square, turned)
    lower = jnp.where(line > lane, square, jnp.where(line < lane, turned, jnp.broadcast_to(pieces[-1][:, :k], (k, k))))
    return upper, lower


def eliminate(table, k, systems):
    lane = lax.broadcasted_iota(jnp.int32, table.shape, 1)
    line = lax.broadcasted_iota(jnp.int32, table.shape, 0)

    def column(step):
        found = jnp.broadcast_to(table[:, step : step + 1], table.shape)
        for s in range(1, systems):
            at = 2 * k * s + step
            found = jnp.where(lane < 2 * k * s, found, jnp.broadcast_to(table[:, at : at + 1], table.shape))
        return found

    for step in range(0, k, 4):
        columns = [column(step + i) for i in range(4)]
        rows = [table[step + i : step + i + 1] for i in range(4)]
        block = [[columns[j][step + i : step + i + 1] for j in range(4)] for i in range(4)]
        (a, b), (c, d) = block[0][:2], block[1][:2]
        scale = 1.0 / (a * d - b * c)

        def upper(x, y):
            return (d * x - b * y) * scale, (a * y - c * x) * scale

        sides = [upper(block[0][j], block[1][j]) for j in (2, 3)]
        first = upper(rows[0], rows[1])
        lower = [[block[i][j] - (block[i][0] * sides[j - 2][0] + block[i][1] * sides[j - 2][1]) for j in (2, 3)] for i in (2, 3)]
        rest = [rows[i] - (block[i][0] * first[0] + block[i][1] * first[1]) for i in (2, 3)]
        scale = 1.0 / (lower[0][0] * lower[1][1] - lower[0][1] * lower[1][0])
        third = (lower[1][1] * rest[0] - lower[0][1] * rest[1]) * scale
        fourth = (lower[0][0] * rest[1] - lower[1][0] * rest[0]) * scale
        new = [first[i] - (sides[0][i] * third + sides[1][i] * fourth) for i in (0, 1)] + [third, fourth]
        table = table - (columns[0] * new[0] + columns[1] * new[1]) - (columns[2] * new[2] + columns[3] * new[3])
        for i in range(4):
            table = jnp.where(line == step + i, new[i], table)
    return table


def odd():
    return lax.rem(lax.axis_index("sx"), 2) == 1


def marks(both):
    rows, face = both.shape
    want = lax.broadcasted_iota(jnp.int32, (face, face), 0).astype(jnp.float32)
    match = jnp.broadcast_to(both[rows - 1 : rows, :], (face, face))
    return jnp.where(want == match, 1.0, 0.0).astype(jnp.bfloat16)


def chosen_kernel(both, chosen):
    chosen[...] = marks(both)


def join_kernel(both, following, residual, rounded):
    k = residual.shape[0]
    face = both.shape[1]
    residual[:, :face] = both[:k, :]
    residual[:, face:] = select(following[:k, :], marks(following), 0)
    rounded[...] = residual[...].astype(jnp.bfloat16)


def near_kernel(size, own, beside, matrix, part, rest, held, sems):
    me = lax.axis_index("sy")
    rows, width = matrix.shape[0], own.shape[1]
    step = min(256, rows)
    copies = []
    for d in range(size):
        columns = pl.ds(pl.multiple_of((me ^ d) * width, width), width)
        target = held.at[d] if d < 2 else rest.at[d - 2]
        copies.append(pltpu.make_async_copy(matrix.at[:, columns], target, sems.at[d]))
        copies[-1].start()
    for d, block in enumerate((own, beside)):
        copies[d].wait()
        for n in range(0, rows, step):
            made = lax.dot_general(
                block[...], held[d, n : n + step, :], (((1,), (1,)), ((), ())), preferred_element_type=jnp.float32
            )
            part[:, n : n + step] = made if d == 0 else part[:, n : n + step] + made
    for d in range(2, size):
        copies[d].wait()


def far_kernel(far, mode, *refs):
    blocks = refs[:far]
    rest, part, weights, chosen = refs[far : far + 4]
    rows = part.shape[1]
    half = rows // 2
    step = min(256, half)
    if mode == "first":
        product, swap_even, swap_odd, tile = refs[far + 4 :]
    elif mode == "both":
        earlier, product, swap_even, swap_odd, out = refs[far + 4 :]
    elif mode == "one":
        product, swap_even, swap_odd, out = refs[far + 4 :]
    else:
        product, passed, out = refs[far + 4 :]
    for n in range(0, rows, step):
        made = part[:, n : n + step]
        for d in range(far):
            made = made + lax.dot_general(
                blocks[d][...], rest[d, n : n + step, :], (((1,), (1,)), ((), ())), preferred_element_type=jnp.float32
            )
        product[:, n : n + step] = made
    if mode == "last":
        passed[...] = product[:, half:]
    else:
        picked = select(product[:, :half], chosen[...], 0)
        right = product[:, half:]
        swap_even[...] = jnp.where(odd(), picked, right)
        swap_odd[...] = jnp.where(odd(), right, picked)
    fresh = gram(weights[...], product[...])
    if mode == "first":
        tile[...] = halved(fresh)
    elif mode == "both":
        for i, row in enumerate(pack_two(earlier[...], halved(fresh))):
            out[:, :, i * LANES : (i + 1) * LANES] = jnp.broadcast_to(row[None], (out.shape[0], 1, LANES))
    else:
        out[...] = jnp.broadcast_to(pack(fresh)[None], out.shape)


def assembled(product, got_even, got_odd, chosen):
    half = product.shape[1] // 2
    from_left = jnp.where(odd(), got_even[...], got_odd[...])
    from_right = jnp.where(odd(), got_odd[...], got_even[...])
    left = product[:, :half] + select(from_left, chosen[...], 1)
    return jnp.concatenate([left, product[:, half:] + from_right], axis=1)


def direction_kernel(product, got_even, got_odd, chosen, search, rounded):
    search[...] = assembled(product, got_even, got_odd, chosen)
    rounded[...] = search[...].astype(jnp.bfloat16)


def alpha_kernel(partials, product, got_even, got_odd, chosen, residual, new_residual, rounded, solved):
    k = residual.shape[0]
    gamma, delta = unpack_two(jnp.sum(partials[...], axis=0), k)
    line, lane = places(k)
    eye = jnp.where(line == lane, 1.0, 0.0).astype(jnp.float32)
    table = eliminate(jnp.concatenate([delta, gamma, gamma, eye], axis=1), k, 2)
    solved[...] = table
    image = assembled(product, got_even, got_odd, chosen)
    new_residual[...] = residual[...] - combine(table[:, k : 2 * k], image)
    rounded[...] = new_residual[...].astype(jnp.bfloat16)


def beta_kernel(partials, product, got_even, got_odd, chosen, search, solved, new_search, rounded, gnew):
    k = search.shape[0]
    fresh = halved(unpack(jnp.sum(partials[...], axis=0), k))
    gnew[...] = fresh
    beta = lax.dot_general(
        solved[:, 3 * k : 4 * k], fresh, (((1,), (0,)), ((), ())), precision=HIGH, preferred_element_type=jnp.float32
    )
    new_search[...] = assembled(product, got_even, got_odd, chosen) + combine(beta, search[...])
    rounded[...] = new_search[...].astype(jnp.bfloat16)


def last_kernel(partials, product, from_left, chosen, residual, search, new_search, solved, gnew, sol, res):
    k = residual.shape[0]
    half = product.shape[1] // 2
    delta = halved(unpack(jnp.sum(partials[...], axis=0), k))
    pad = jnp.zeros((k, LANES - 2 * k), jnp.float32)
    table = eliminate(jnp.concatenate([delta, gnew[...], pad], axis=1), k, 1)
    alpha = table[:, k : 2 * k]
    left = product[:, :half] + select(from_left[...], chosen[...], 1)
    res[...] = residual[:, :half] - combine(alpha, left)
    sol[...] = combine(solved[:, k : 2 * k], search[:, :half]) + combine(alpha, new_search[:, :half])


def spread(partials):
    return lax.all_to_all(partials, AXES, 0, 0)


def shards(schur, precond, right_side, matching):
    schur_rows = schur[0]
    precond_rows = precond[0]
    start = right_side[0]
    k, face = start.shape
    size = lax.axis_size("sy")
    count = lax.axis_size("sx") * size
    tile_rows = k * k // LANES
    above = lax.pad(start, jnp.float32(0), ((0, 1, 0), (0, 0, 0)))
    below = lax.pad(matching, jnp.int32(0), ((k, 0, 0), (0, 0, 0)))
    both = above + below.astype(jnp.float32)
    following = passed_along(both, -1)
    chosen = call(chosen_kernel, bf16(face, face), both)

    def apply(rounded, matrix, weights, mode, *earlier):
        far = [partner(rounded, d) for d in range(2, size)]
        beside = partner(rounded, 1)
        rows, width = matrix.shape[0], rounded.shape[1]
        room = 2 * matrix.size + (4 << 20)
        part, rest = call(
            functools.partial(near_kernel, size), (f32(k, rows), bf16(size - 2, rows, width)), rounded, beside, matrix,
            places=[VMEM, VMEM, pl.BlockSpec(memory_space=pltpu.HBM)],
            scratch=(pltpu.VMEM((2, rows, width), jnp.bfloat16), pltpu.SemaphoreType.DMA((size,))),
            room=BUDGET - matrix.size * 7 // 4,
        )
        swap = (f32(k, face), f32(k, face))
        outs = {
            "first": (f32(k, rows), *swap, f32(k, k)),
            "both": (f32(k, rows), *swap, f32(count, 1, (tile_rows + 1) * LANES)),
            "one": (f32(k, rows), *swap, f32(count, tile_rows, LANES)),
            "last": (f32(k, rows), f32(k, face), f32(count, tile_rows, LANES)),
        }[mode]
        return call(
            functools.partial(far_kernel, len(far), mode), outs, *far, rest, part, weights, chosen, *earlier, room=room
        )

    vectors = (f32(k, 2 * face), bf16(k, 2 * face))
    residual, rounded = call(join_kernel, vectors, both, following)
    product, even, odd_, tile = apply(rounded, precond_rows, residual, "first")
    got_odd, got_even = swapped(odd_, 1), swapped(even, 0)
    search, rounded = call(direction_kernel, vectors, product, got_even, got_odd, chosen)

    product, even, odd_, partials = apply(rounded, schur_rows, search, "both", tile)
    partials = spread(partials)
    got_odd, got_even = swapped(odd_, 1), swapped(even, 0)
    residual, rounded, solved = call(
        alpha_kernel, (*vectors, f32(k, LANES)), partials, product, got_even, got_odd, chosen, residual
    )

    product, even, odd_, partials = apply(rounded, precond_rows, residual, "one")
    partials = spread(partials)
    got_odd, got_even = swapped(odd_, 1), swapped(even, 0)
    new_search, rounded, gnew = call(
        beta_kernel, (*vectors, f32(k, k)), partials, product, got_even, got_odd, chosen, search, solved
    )

    product, passed, partials = apply(rounded, schur_rows, new_search, "last")
    partials = spread(partials)
    from_left = passed_along(passed, 1)
    sol, res = call(
        last_kernel, (f32(k, face), f32(k, face)),
        partials, product, from_left, chosen, residual, search, new_search, solved, gnew,
    )
    return (sol[None], res[None])


def solution(mesh):
    in_specs = (P("sx", "sy", None), P("sx", "sy", None), P("sx", None, "sy"), P("sx", "sy"))
    out_specs = (P("sx", None, "sy"), P("sx", None, "sy"))
    return jax.shard_map(shards, mesh=mesh, in_specs=in_specs, out_specs=out_specs, check_vma=False)
```

```python
import functools

import jax
import jax.numpy as jnp
from jax import lax
from jax.experimental import pallas as pl
from jax.experimental.pallas import tpu as pltpu
from jax.sharding import PartitionSpec as P


LANES = 128
BUDGET = 55 << 20
AXES = ("sx", "sy")
HIGH = lax.Precision.HIGHEST
VMEM = pl.BlockSpec(memory_space=pltpu.VMEM)


def call(body, outs, *args, places=None, scratch=(), room=0):
    room = room or (4 << 20) + sum(2 * a.size * a.dtype.itemsize for a in args if a.ndim == 3)
    return pl.pallas_call(
        body,
        out_shape=outs,
        in_specs=places or [VMEM] * len(args),
        out_specs=jax.tree.map(lambda _: VMEM, outs),
        scratch_shapes=scratch,
        cost_estimate=pl.CostEstimate(flops=1 << 24, bytes_accessed=1 << 23, transcendentals=0),
        compiler_params=pltpu.CompilerParams(vmem_limit_bytes=room),
    )(*args)


def f32(*shape):
    return jax.ShapeDtypeStruct(shape, jnp.float32)


def bf16(*shape):
    return jax.ShapeDtypeStruct(shape, jnp.bfloat16)


def passed_along(block, distance):
    devices = range(lax.axis_size("sx"))
    route = [((i - distance) % len(devices), i) for i in devices]
    return lax.ppermute(block, "sx", route)


def swapped(block, first):
    n = lax.axis_size("sx")
    route = []
    for i in range(first, n, 2):
        j = (i + 1) % n
        route += [(i, j), (j, i)]
    return lax.ppermute(block, "sx", route)


def partner(block, distance):
    return lax.ppermute(block, "sy", [(i, i ^ distance) for i in range(lax.axis_size("sy"))])


def select(value, chosen, axis):
    k = value.shape[0]
    high = value.astype(jnp.bfloat16)
    rest = value - high.astype(jnp.float32)
    mid = rest.astype(jnp.bfloat16)
    low = (rest - mid.astype(jnp.float32)).astype(jnp.bfloat16)
    pieces = jnp.concatenate([high, mid, low], axis=0)
    picked = lax.dot_general(pieces, chosen, (((1,), (axis,)), ((), ())), preferred_element_type=jnp.float32)
    return (picked[:k] + picked[k : 2 * k]) + picked[2 * k :]


def gram(first, second):
    return lax.dot_general(first, second, (((1,), (1,)), ((), ())), precision=HIGH, preferred_element_type=jnp.float32)


def combine(coeff, block):
    return lax.dot_general(coeff, block, (((0,), (0,)), ((), ())), precision=HIGH, preferred_element_type=jnp.float32)


def pack(square):
    k = square.shape[0]
    pieces = LANES // k
    rows = k // pieces
    return jnp.concatenate([square[i * rows : (i + 1) * rows] for i in range(pieces)], axis=1)


def unpack(tile, k):
    pieces = LANES // k
    return jnp.concatenate([tile[:, i * k : (i + 1) * k] for i in range(pieces)], axis=0)


def halved(square):
    return 0.5 * (square + square.T)


def places(k):
    return lax.broadcasted_iota(jnp.int32, (k, k), 0), lax.broadcasted_iota(jnp.int32, (k, k), 1)


def pack_two(upper, lower):
    k = upper.shape[0]
    line, lane = places(k)
    tile = pack(jnp.where(line <= lane, upper, lower))
    diagonal = jnp.sum(jnp.where(line == lane, lower, 0.0), axis=0, keepdims=True)
    pad = jnp.zeros((1, LANES - k), jnp.float32)
    return [tile[i : i + 1] for i in range(tile.shape[0])] + [jnp.concatenate([diagonal, pad], axis=1)]


def unpack_two(row, k):
    line, lane = places(k)
    pieces = [row[:, i : i + LANES] for i in range(0, row.shape[1], LANES)]
    square = unpack(jnp.concatenate(pieces[:-1], axis=0), k)
    turned = square.T
    upper = jnp.where(line <= lane, square, turned)
    lower = jnp.where(line > lane, square, jnp.where(line < lane, turned, jnp.broadcast_to(pieces[-1][:, :k], (k, k))))
    return upper, lower


def solved(matrix, sides):
    k = matrix.shape[0]
    table = jnp.concatenate([matrix, sides, jnp.zeros((k, LANES - 2 * k), jnp.float32)], axis=1)
    line = lax.broadcasted_iota(jnp.int32, table.shape, 0)
    for step in range(0, k, 4):
        columns = [jnp.broadcast_to(table[:, step + i : step + i + 1], table.shape) for i in range(4)]
        rows = [table[step + i : step + i + 1] for i in range(4)]
        block = [[columns[j][step + i : step + i + 1] for j in range(4)] for i in range(4)]
        (a, b), (c, d) = block[0][:2], block[1][:2]
        scale = 1.0 / (a * d - b * c)

        def upper(x, y):
            return (d * x - b * y) * scale, (a * y - c * x) * scale

        sides = [upper(block[0][j], block[1][j]) for j in (2, 3)]
        first = upper(rows[0], rows[1])
        lower = [[block[i][j] - (block[i][0] * sides[j - 2][0] + block[i][1] * sides[j - 2][1]) for j in (2, 3)] for i in (2, 3)]
        rest = [rows[i] - (block[i][0] * first[0] + block[i][1] * first[1]) for i in (2, 3)]
        scale = 1.0 / (lower[0][0] * lower[1][1] - lower[0][1] * lower[1][0])
        third = (lower[1][1] * rest[0] - lower[0][1] * rest[1]) * scale
        fourth = (lower[0][0] * rest[1] - lower[1][0] * rest[0]) * scale
        new = [first[i] - (sides[0][i] * third + sides[1][i] * fourth) for i in (0, 1)] + [third, fourth]
        table = table - (columns[0] * new[0] + columns[1] * new[1]) - (columns[2] * new[2] + columns[3] * new[3])
        for i in range(4):
            table = jnp.where(line == step + i, new[i], table)
    return table[:, k : 2 * k]


def odd():
    return lax.rem(lax.axis_index("sx"), 2) == 1


def marks(both):
    rows, face = both.shape
    want = lax.broadcasted_iota(jnp.int32, (face, face), 0).astype(jnp.float32)
    match = jnp.broadcast_to(both[rows - 1 : rows, :], (face, face))
    return jnp.where(want == match, 1.0, 0.0).astype(jnp.bfloat16)


def chosen_kernel(both, chosen):
    chosen[...] = marks(both)


def join_kernel(both, following, residual, rounded):
    k = residual.shape[0]
    face = both.shape[1]
    residual[:, :face] = both[:k, :]
    residual[:, face:] = select(following[:k, :], marks(following), 0)
    rounded[...] = residual[...].astype(jnp.bfloat16)


def near_kernel(size, own, beside, matrix, part, rest, held, sems):
    me = lax.axis_index("sy")
    rows, width = matrix.shape[0], own.shape[1]
    step = min(256, rows)
    copies = []
    for d in range(size):
        columns = pl.ds(pl.multiple_of((me ^ d) * width, width), width)
        target = held.at[d] if d < 2 else rest.at[d - 2]
        copies.append(pltpu.make_async_copy(matrix.at[:, columns], target, sems.at[d]))
        copies[-1].start()
    for d, block in enumerate((own, beside)):
        copies[d].wait()
        for n in range(0, rows, step):
            made = lax.dot_general(
                block[...], held[d, n : n + step, :], (((1,), (1,)), ((), ())), preferred_element_type=jnp.float32
            )
            part[:, n : n + step] = made if d == 0 else part[:, n : n + step] + made
    for d in range(2, size):
        copies[d].wait()


def far_kernel(far, mode, *refs):
    blocks = refs[:far]
    rest, part, weights, chosen = refs[far : far + 4]
    rows = part.shape[1]
    half = rows // 2
    step = min(256, half)
    if mode == "first":
        product, swap_even, swap_odd, tile = refs[far + 4 :]
    elif mode == "both":
        earlier, product, swap_even, swap_odd, out = refs[far + 4 :]
    elif mode == "one":
        product, swap_even, swap_odd, out = refs[far + 4 :]
    else:
        product, passed, out = refs[far + 4 :]
    for n in range(0, rows, step):
        made = part[:, n : n + step]
        for d in range(far):
            made = made + lax.dot_general(
                blocks[d][...], rest[d, n : n + step, :], (((1,), (1,)), ((), ())), preferred_element_type=jnp.float32
            )
        product[:, n : n + step] = made
    if mode == "last":
        passed[...] = product[:, half:]
    else:
        picked = select(product[:, :half], chosen[...], 0)
        right = product[:, half:]
        swap_even[...] = jnp.where(odd(), picked, right)
        swap_odd[...] = jnp.where(odd(), right, picked)
    fresh = gram(weights[...], product[...])
    if mode == "first":
        tile[...] = halved(fresh)
    elif mode == "both":
        for i, row in enumerate(pack_two(earlier[...], halved(fresh))):
            out[:, :, i * LANES : (i + 1) * LANES] = jnp.broadcast_to(row[None], (out.shape[0], 1, LANES))
    else:
        out[...] = jnp.broadcast_to(pack(fresh)[None], out.shape)


def assembled(product, got_even, got_odd, chosen):
    half = product.shape[1] // 2
    from_left = jnp.where(odd(), got_even[...], got_odd[...])
    from_right = jnp.where(odd(), got_odd[...], got_even[...])
    left = product[:, :half] + select(from_left, chosen[...], 1)
    return jnp.concatenate([left, product[:, half:] + from_right], axis=1)


def direction_kernel(product, got_even, got_odd, chosen, search, rounded):
    search[...] = assembled(product, got_even, got_odd, chosen)
    rounded[...] = search[...].astype(jnp.bfloat16)


def alpha_kernel(partials, alpha, gamma):
    gamma[...], delta = unpack_two(jnp.sum(partials[...], axis=0), alpha.shape[0])
    alpha[...] = solved(delta, gamma[...])


def residual_kernel(alpha, product, got_even, got_odd, chosen, residual, new_residual, rounded):
    image = assembled(product, got_even, got_odd, chosen)
    new_residual[...] = residual[...] - combine(alpha[...], image)
    rounded[...] = new_residual[...].astype(jnp.bfloat16)


def aside_kernel(gamma, alpha, search, inverse, moved):
    k, half = moved.shape
    line, lane = places(k)
    inverse[...] = solved(gamma[...], jnp.where(line == lane, 1.0, 0.0).astype(jnp.float32))
    moved[...] = combine(alpha[...], search[:, :half])


def beta_kernel(partials, inverse, beta, gnew):
    gnew[...] = halved(unpack(jnp.sum(partials[...], axis=0), gnew.shape[0]))
    beta[...] = lax.dot_general(
        inverse[...], gnew[...], (((1,), (0,)), ((), ())), precision=HIGH, preferred_element_type=jnp.float32
    )


def search_kernel(beta, product, got_even, got_odd, chosen, search, new_search, rounded):
    new_search[...] = assembled(product, got_even, got_odd, chosen) + combine(beta[...], search[...])
    rounded[...] = new_search[...].astype(jnp.bfloat16)


def last_alpha_kernel(partials, gnew, alpha):
    delta = halved(unpack(jnp.sum(partials[...], axis=0), alpha.shape[0]))
    alpha[...] = solved(delta, gnew[...])


def last_kernel(alpha, product, from_left, chosen, residual, moved, new_search, sol, res):
    half = product.shape[1] // 2
    left = product[:, :half] + select(from_left[...], chosen[...], 1)
    res[...] = residual[:, :half] - combine(alpha[...], left)
    sol[...] = moved[...] + combine(alpha[...], new_search[:, :half])


def spread(partials):
    return lax.all_to_all(partials, AXES, 0, 0)


def shards(schur, precond, right_side, matching):
    schur_rows = schur[0]
    precond_rows = precond[0]
    start = right_side[0]
    k, face = start.shape
    size = lax.axis_size("sy")
    count = lax.axis_size("sx") * size
    tile_rows = k * k // LANES
    above = lax.pad(start, jnp.float32(0), ((0, 1, 0), (0, 0, 0)))
    below = lax.pad(matching, jnp.int32(0), ((k, 0, 0), (0, 0, 0)))
    both = above + below.astype(jnp.float32)
    following = passed_along(both, -1)
    chosen = call(chosen_kernel, bf16(face, face), both)

    def apply(rounded, matrix, weights, mode, *earlier):
        far = [partner(rounded, d) for d in range(2, size)]
        beside = partner(rounded, 1)
        rows, width = matrix.shape[0], rounded.shape[1]
        room = 2 * matrix.size + (4 << 20)
        part, rest = call(
            functools.partial(near_kernel, size), (f32(k, rows), bf16(size - 2, rows, width)), rounded, beside, matrix,
            places=[VMEM, VMEM, pl.BlockSpec(memory_space=pltpu.HBM)],
            scratch=(pltpu.VMEM((2, rows, width), jnp.bfloat16), pltpu.SemaphoreType.DMA((size,))),
            room=BUDGET - matrix.size * 7 // 4,
        )
        swap = (f32(k, face), f32(k, face))
        outs = {
            "first": (f32(k, rows), *swap, f32(k, k)),
            "both": (f32(k, rows), *swap, f32(count, 1, (tile_rows + 1) * LANES)),
            "one": (f32(k, rows), *swap, f32(count, tile_rows, LANES)),
            "last": (f32(k, rows), f32(k, face), f32(count, tile_rows, LANES)),
        }[mode]
        return call(
            functools.partial(far_kernel, len(far), mode), outs, *far, rest, part, weights, chosen, *earlier, room=room
        )

    vectors = (f32(k, 2 * face), bf16(k, 2 * face))
    residual, rounded = call(join_kernel, vectors, both, following)
    product, even, odd_, tile = apply(rounded, precond_rows, residual, "first")
    got_odd, got_even = swapped(odd_, 1), swapped(even, 0)
    search, rounded = call(direction_kernel, vectors, product, got_even, got_odd, chosen)

    product, even, odd_, partials = apply(rounded, schur_rows, search, "both", tile)
    partials = spread(partials)
    got_odd, got_even = swapped(odd_, 1), swapped(even, 0)
    alpha, gamma = call(alpha_kernel, (f32(k, k), f32(k, k)), partials)
    residual, rounded = call(residual_kernel, vectors, alpha, product, got_even, got_odd, chosen, residual)

    inverse, moved = call(aside_kernel, (f32(k, k), f32(k, face)), gamma, alpha, search)
    product, even, odd_, partials = apply(rounded, precond_rows, residual, "one")
    partials = spread(partials)
    got_odd, got_even = swapped(odd_, 1), swapped(even, 0)
    beta, gnew = call(beta_kernel, (f32(k, k), f32(k, k)), partials, inverse)
    new_search, rounded = call(search_kernel, vectors, beta, product, got_even, got_odd, chosen, search)

    product, passed, partials = apply(rounded, schur_rows, new_search, "last")
    partials = spread(partials)
    from_left = passed_along(passed, 1)
    alpha = call(last_alpha_kernel, f32(k, k), partials, gnew)
    sol, res = call(
        last_kernel, (f32(k, face), f32(k, face)),
        alpha, product, from_left, chosen, residual, moved, new_search,
    )
    return (sol[None], res[None])


def solution(mesh):
    in_specs = (P("sx", "sy", None), P("sx", "sy", None), P("sx", None, "sy"), P("sx", "sy"))
    out_specs = (P("sx", None, "sy"), P("sx", None, "sy"))
    return jax.shard_map(shards, mesh=mesh, in_specs=in_specs, out_specs=out_specs, check_vma=False)
```

```python
import functools

import jax
import jax.numpy as jnp
from jax import lax
from jax.experimental import pallas as pl
from jax.experimental.pallas import tpu as pltpu
from jax.sharding import PartitionSpec as P


LANES = 128
BUDGET = 55 << 20
AXES = ("sx", "sy")
HIGH = lax.Precision.HIGHEST
VMEM = pl.BlockSpec(memory_space=pltpu.VMEM)


def call(body, outs, *args, places=None, scratch=(), room=0):
    room = room or (4 << 20) + sum(2 * a.size * a.dtype.itemsize for a in args if a.ndim == 3)
    return pl.pallas_call(
        body,
        out_shape=outs,
        in_specs=places or [VMEM] * len(args),
        out_specs=jax.tree.map(lambda _: VMEM, outs),
        scratch_shapes=scratch,
        cost_estimate=pl.CostEstimate(flops=1 << 24, bytes_accessed=1 << 23, transcendentals=0),
        compiler_params=pltpu.CompilerParams(vmem_limit_bytes=room),
    )(*args)


def f32(*shape):
    return jax.ShapeDtypeStruct(shape, jnp.float32)


def bf16(*shape):
    return jax.ShapeDtypeStruct(shape, jnp.bfloat16)


def passed_along(block, distance):
    devices = range(lax.axis_size("sx"))
    route = [((i - distance) % len(devices), i) for i in devices]
    return lax.ppermute(block, "sx", route)


def swapped(block, first):
    n = lax.axis_size("sx")
    route = []
    for i in range(first, n, 2):
        j = (i + 1) % n
        route += [(i, j), (j, i)]
    return lax.ppermute(block, "sx", route)


def partner(block, distance):
    return lax.ppermute(block, "sy", [(i, i ^ distance) for i in range(lax.axis_size("sy"))])


def select(value, chosen, axis):
    k = value.shape[0]
    high = value.astype(jnp.bfloat16)
    rest = value - high.astype(jnp.float32)
    mid = rest.astype(jnp.bfloat16)
    low = (rest - mid.astype(jnp.float32)).astype(jnp.bfloat16)
    pieces = jnp.concatenate([high, mid, low], axis=0)
    picked = lax.dot_general(pieces, chosen, (((1,), (axis,)), ((), ())), preferred_element_type=jnp.float32)
    return (picked[:k] + picked[k : 2 * k]) + picked[2 * k :]


def gram(first, second):
    return lax.dot_general(first, second, (((1,), (1,)), ((), ())), precision=HIGH, preferred_element_type=jnp.float32)


def combine(coeff, block):
    return lax.dot_general(coeff, block, (((0,), (0,)), ((), ())), precision=HIGH, preferred_element_type=jnp.float32)


def pack(square):
    k = square.shape[0]
    pieces = LANES // k
    rows = k // pieces
    return jnp.concatenate([square[i * rows : (i + 1) * rows] for i in range(pieces)], axis=1)


def unpack(tile, k):
    pieces = LANES // k
    return jnp.concatenate([tile[:, i * k : (i + 1) * k] for i in range(pieces)], axis=0)


def halved(square):
    return 0.5 * (square + square.T)


def places(k):
    return lax.broadcasted_iota(jnp.int32, (k, k), 0), lax.broadcasted_iota(jnp.int32, (k, k), 1)


def pack_two(upper, lower):
    k = upper.shape[0]
    line, lane = places(k)
    tile = pack(jnp.where(line <= lane, upper, lower))
    diagonal = jnp.sum(jnp.where(line == lane, lower, 0.0), axis=0, keepdims=True)
    pad = jnp.zeros((1, LANES - k), jnp.float32)
    return [tile[i : i + 1] for i in range(tile.shape[0])] + [jnp.concatenate([diagonal, pad], axis=1)]


def unpack_two(row, k):
    line, lane = places(k)
    pieces = [row[:, i : i + LANES] for i in range(0, row.shape[1], LANES)]
    square = unpack(jnp.concatenate(pieces[:-1], axis=0), k)
    turned = square.T
    upper = jnp.where(line <= lane, square, turned)
    lower = jnp.where(line > lane, square, jnp.where(line < lane, turned, jnp.broadcast_to(pieces[-1][:, :k], (k, k))))
    return upper, lower


def pair(a, b, c, d):
    over_a = 1.0 / a
    ratio = b * over_a
    over_d = 1.0 / (d - c * ratio)

    def solve(x, y):
        x = x * over_a
        y = (y - c * x) * over_d
        return x - ratio * y, y

    return solve


def solved(matrix, sides):
    k = matrix.shape[0]
    table = jnp.concatenate([matrix, sides, jnp.zeros((k, LANES - 2 * k), jnp.float32)], axis=1)
    line = lax.broadcasted_iota(jnp.int32, table.shape, 0)
    for step in range(0, k, 4):
        columns = [jnp.broadcast_to(table[:, step + i : step + i + 1], table.shape) for i in range(4)]
        rows = [table[step + i : step + i + 1] for i in range(4)]
        block = [[columns[j][step + i : step + i + 1] for j in range(4)] for i in range(4)]
        upper = pair(*block[0][:2], *block[1][:2])
        sides = [upper(block[0][j], block[1][j]) for j in (2, 3)]
        first = upper(rows[0], rows[1])
        lower = [
            [block[i][j] - (block[i][0] * sides[j - 2][0] + block[i][1] * sides[j - 2][1]) for j in (2, 3)]
            for i in (2, 3)
        ]
        rest = [rows[i] - (block[i][0] * first[0] + block[i][1] * first[1]) for i in (2, 3)]
        third, fourth = pair(*lower[0], *lower[1])(*rest)
        new = [first[i] - (sides[0][i] * third + sides[1][i] * fourth) for i in (0, 1)] + [third, fourth]
        table = table - (columns[0] * new[0] + columns[1] * new[1]) - (columns[2] * new[2] + columns[3] * new[3])
        for i in range(4):
            table = jnp.where(line == step + i, new[i], table)
    return table[:, k : 2 * k]


def odd():
    return lax.rem(lax.axis_index("sx"), 2) == 1


def marks(both):
    rows, face = both.shape
    want = lax.broadcasted_iota(jnp.int32, (face, face), 0).astype(jnp.float32)
    match = jnp.broadcast_to(both[rows - 1 : rows, :], (face, face))
    return jnp.where(want == match, 1.0, 0.0).astype(jnp.bfloat16)


def chosen_kernel(both, chosen):
    chosen[...] = marks(both)


def join_kernel(both, following, residual, rounded):
    k = residual.shape[0]
    face = both.shape[1]
    residual[:, :face] = both[:k, :]
    residual[:, face:] = select(following[:k, :], marks(following), 0)
    rounded[...] = residual[...].astype(jnp.bfloat16)


def near_kernel(size, own, beside, matrix, part, rest, held, sems):
    me = lax.axis_index("sy")
    rows, width = matrix.shape[0], own.shape[1]
    step = min(256, rows)
    copies = []
    for d in range(size):
        columns = pl.ds(pl.multiple_of((me ^ d) * width, width), width)
        target = held.at[d] if d < 2 else rest.at[d - 2]
        copies.append(pltpu.make_async_copy(matrix.at[:, columns], target, sems.at[d]))
        copies[-1].start()
    for d, block in enumerate((own, beside)):
        copies[d].wait()
        for n in range(0, rows, step):
            made = lax.dot_general(
                block[...], held[d, n : n + step, :], (((1,), (1,)), ((), ())), preferred_element_type=jnp.float32
            )
            part[:, n : n + step] = made if d == 0 else part[:, n : n + step] + made
    for d in range(2, size):
        copies[d].wait()


def far_kernel(far, mode, *refs):
    blocks = refs[:far]
    rest, part, weights, chosen = refs[far : far + 4]
    rows = part.shape[1]
    half = rows // 2
    step = min(256, half)
    if mode == "first":
        product, swap_even, swap_odd, tile = refs[far + 4 :]
    elif mode == "both":
        earlier, product, swap_even, swap_odd, out = refs[far + 4 :]
    elif mode == "one":
        product, swap_even, swap_odd, out = refs[far + 4 :]
    else:
        product, passed, out = refs[far + 4 :]
    for n in range(0, rows, step):
        made = part[:, n : n + step]
        for d in range(far):
            made = made + lax.dot_general(
                blocks[d][...], rest[d, n : n + step, :], (((1,), (1,)), ((), ())), preferred_element_type=jnp.float32
            )
        product[:, n : n + step] = made
    if mode == "last":
        passed[...] = product[:, half:]
    else:
        picked = select(product[:, :half], chosen[...], 0)
        right = product[:, half:]
        swap_even[...] = jnp.where(odd(), picked, right)
        swap_odd[...] = jnp.where(odd(), right, picked)
    fresh = gram(weights[...], product[...])
    if mode == "first":
        tile[...] = halved(fresh)
    elif mode == "both":
        for i, row in enumerate(pack_two(earlier[...], halved(fresh))):
            out[:, :, i * LANES : (i + 1) * LANES] = jnp.broadcast_to(row[None], (out.shape[0], 1, LANES))
    else:
        out[...] = jnp.broadcast_to(pack(fresh)[None], out.shape)


def assembled(product, got_even, got_odd, chosen):
    half = product.shape[1] // 2
    from_left = jnp.where(odd(), got_even[...], got_odd[...])
    from_right = jnp.where(odd(), got_odd[...], got_even[...])
    left = product[:, :half] + select(from_left, chosen[...], 1)
    return jnp.concatenate([left, product[:, half:] + from_right], axis=1)


def direction_kernel(product, got_even, got_odd, chosen, search, rounded):
    search[...] = assembled(product, got_even, got_odd, chosen)
    rounded[...] = search[...].astype(jnp.bfloat16)


def alpha_kernel(partials, alpha, gamma):
    gamma[...], delta = unpack_two(jnp.sum(partials[...], axis=0), alpha.shape[0])
    alpha[...] = solved(delta, gamma[...])


def residual_kernel(alpha, product, got_even, got_odd, chosen, residual, new_residual, rounded):
    image = assembled(product, got_even, got_odd, chosen)
    new_residual[...] = residual[...] - combine(alpha[...], image)
    rounded[...] = new_residual[...].astype(jnp.bfloat16)


def aside_kernel(gamma, alpha, search, inverse, moved):
    k, half = moved.shape
    line, lane = places(k)
    inverse[...] = solved(gamma[...], jnp.where(line == lane, 1.0, 0.0).astype(jnp.float32))
    moved[...] = combine(alpha[...], search[:, :half])


def beta_kernel(partials, inverse, beta, gnew):
    gnew[...] = halved(unpack(jnp.sum(partials[...], axis=0), gnew.shape[0]))
    beta[...] = lax.dot_general(
        inverse[...], gnew[...], (((1,), (0,)), ((), ())), precision=HIGH, preferred_element_type=jnp.float32
    )


def search_kernel(beta, product, got_even, got_odd, chosen, search, new_search, rounded):
    new_search[...] = assembled(product, got_even, got_odd, chosen) + combine(beta[...], search[...])
    rounded[...] = new_search[...].astype(jnp.bfloat16)


def last_alpha_kernel(partials, gnew, alpha):
    delta = halved(unpack(jnp.sum(partials[...], axis=0), alpha.shape[0]))
    alpha[...] = solved(delta, gnew[...])


def last_kernel(alpha, product, from_left, chosen, residual, moved, new_search, sol, res):
    half = product.shape[1] // 2
    left = product[:, :half] + select(from_left[...], chosen[...], 1)
    res[...] = residual[:, :half] - combine(alpha[...], left)
    sol[...] = moved[...] + combine(alpha[...], new_search[:, :half])


def spread(partials):
    return lax.all_to_all(partials, AXES, 0, 0)


def shards(schur, precond, right_side, matching):
    schur_rows = schur[0]
    precond_rows = precond[0]
    start = right_side[0]
    k, face = start.shape
    size = lax.axis_size("sy")
    count = lax.axis_size("sx") * size
    tile_rows = k * k // LANES
    above = lax.pad(start, jnp.float32(0), ((0, 1, 0), (0, 0, 0)))
    below = lax.pad(matching, jnp.int32(0), ((k, 0, 0), (0, 0, 0)))
    both = above + below.astype(jnp.float32)
    following = passed_along(both, -1)
    chosen = call(chosen_kernel, bf16(face, face), both)

    def apply(rounded, matrix, weights, mode, *earlier):
        far = [partner(rounded, d) for d in range(2, size)]
        beside = partner(rounded, 1)
        rows, width = matrix.shape[0], rounded.shape[1]
        room = 2 * matrix.size + (4 << 20)
        part, rest = call(
            functools.partial(near_kernel, size), (f32(k, rows), bf16(size - 2, rows, width)), rounded, beside, matrix,
            places=[VMEM, VMEM, pl.BlockSpec(memory_space=pltpu.HBM)],
            scratch=(pltpu.VMEM((2, rows, width), jnp.bfloat16), pltpu.SemaphoreType.DMA((size,))),
            room=BUDGET - matrix.size * 7 // 4,
        )
        swap = (f32(k, face), f32(k, face))
        outs = {
            "first": (f32(k, rows), *swap, f32(k, k)),
            "both": (f32(k, rows), *swap, f32(count, 1, (tile_rows + 1) * LANES)),
            "one": (f32(k, rows), *swap, f32(count, tile_rows, LANES)),
            "last": (f32(k, rows), f32(k, face), f32(count, tile_rows, LANES)),
        }[mode]
        return call(
            functools.partial(far_kernel, len(far), mode), outs, *far, rest, part, weights, chosen, *earlier, room=room
        )

    vectors = (f32(k, 2 * face), bf16(k, 2 * face))
    residual, rounded = call(join_kernel, vectors, both, following)
    product, even, odd_, tile = apply(rounded, precond_rows, residual, "first")
    got_odd, got_even = swapped(odd_, 1), swapped(even, 0)
    search, rounded = call(direction_kernel, vectors, product, got_even, got_odd, chosen)

    product, even, odd_, partials = apply(rounded, schur_rows, search, "both", tile)
    partials = spread(partials)
    got_odd, got_even = swapped(odd_, 1), swapped(even, 0)
    alpha, gamma = call(alpha_kernel, (f32(k, k), f32(k, k)), partials)
    residual, rounded = call(residual_kernel, vectors, alpha, product, got_even, got_odd, chosen, residual)

    inverse, moved = call(aside_kernel, (f32(k, k), f32(k, face)), gamma, alpha, search)
    product, even, odd_, partials = apply(rounded, precond_rows, residual, "one")
    partials = spread(partials)
    got_odd, got_even = swapped(odd_, 1), swapped(even, 0)
    beta, gnew = call(beta_kernel, (f32(k, k), f32(k, k)), partials, inverse)
    new_search, rounded = call(search_kernel, vectors, beta, product, got_even, got_odd, chosen, search)

    product, passed, partials = apply(rounded, schur_rows, new_search, "last")
    partials = spread(partials)
    from_left = passed_along(passed, 1)
    alpha = call(last_alpha_kernel, f32(k, k), partials, gnew)
    sol, res = call(
        last_kernel, (f32(k, face), f32(k, face)),
        alpha, product, from_left, chosen, residual, moved, new_search,
    )
    return (sol[None], res[None])


def solution(mesh):
    in_specs = (P("sx", "sy", None), P("sx", "sy", None), P("sx", None, "sy"), P("sx", "sy"))
    out_specs = (P("sx", None, "sy"), P("sx", None, "sy"))
    return jax.shard_map(shards, mesh=mesh, in_specs=in_specs, out_specs=out_specs, check_vma=False)
```

```python
import functools

import jax
import jax.numpy as jnp
from jax import lax
from jax.experimental import pallas as pl
from jax.experimental.pallas import tpu as pltpu
from jax.sharding import PartitionSpec as P


LANES = 128
BUDGET = 55 << 20
AXES = ("sx", "sy")
HIGH = lax.Precision.HIGHEST
VMEM = pl.BlockSpec(memory_space=pltpu.VMEM)


def call(body, outs, *args, places=None, scratch=(), room=0):
    room = room or (4 << 20) + sum(2 * a.size * a.dtype.itemsize for a in args if a.ndim == 3)
    return pl.pallas_call(
        body,
        out_shape=outs,
        in_specs=places or [VMEM] * len(args),
        out_specs=jax.tree.map(lambda _: VMEM, outs),
        scratch_shapes=scratch,
        cost_estimate=pl.CostEstimate(flops=1 << 24, bytes_accessed=1 << 23, transcendentals=0),
        compiler_params=pltpu.CompilerParams(vmem_limit_bytes=room),
    )(*args)


def f32(*shape):
    return jax.ShapeDtypeStruct(shape, jnp.float32)


def bf16(*shape):
    return jax.ShapeDtypeStruct(shape, jnp.bfloat16)


def passed_along(block, distance):
    devices = range(lax.axis_size("sx"))
    route = [((i - distance) % len(devices), i) for i in devices]
    return lax.ppermute(block, "sx", route)


def traded(odd_block, even_block):
    got_even = swapped(even_block, 0)
    got_odd = swapped(odd_block, 1)
    return got_even, got_odd


def swapped(block, first):
    n = lax.axis_size("sx")
    route = []
    for i in range(first, n, 2):
        j = (i + 1) % n
        route += [(i, j), (j, i)]
    return lax.ppermute(block, "sx", route)


def partner(block, distance):
    return lax.ppermute(block, "sy", [(i, i ^ distance) for i in range(lax.axis_size("sy"))])


def select(value, chosen, axis):
    k = value.shape[0]
    high = value.astype(jnp.bfloat16)
    rest = value - high.astype(jnp.float32)
    mid = rest.astype(jnp.bfloat16)
    low = (rest - mid.astype(jnp.float32)).astype(jnp.bfloat16)
    pieces = jnp.concatenate([high, mid, low], axis=0)
    picked = lax.dot_general(pieces, chosen, (((1,), (axis,)), ((), ())), preferred_element_type=jnp.float32)
    return (picked[:k] + picked[k : 2 * k]) + picked[2 * k :]


def gram(first, second):
    return lax.dot_general(first, second, (((1,), (1,)), ((), ())), precision=HIGH, preferred_element_type=jnp.float32)


def combine(coeff, block):
    return lax.dot_general(coeff, block, (((0,), (0,)), ((), ())), precision=HIGH, preferred_element_type=jnp.float32)


def pack(square):
    k = square.shape[0]
    pieces = LANES // k
    rows = k // pieces
    return jnp.concatenate([square[i * rows : (i + 1) * rows] for i in range(pieces)], axis=1)


def unpack(tile, k):
    pieces = LANES // k
    return jnp.concatenate([tile[:, i * k : (i + 1) * k] for i in range(pieces)], axis=0)


def halved(square):
    return 0.5 * (square + square.T)


def places(k):
    return lax.broadcasted_iota(jnp.int32, (k, k), 0), lax.broadcasted_iota(jnp.int32, (k, k), 1)


def pack_two(upper, lower):
    k = upper.shape[0]
    line, lane = places(k)
    tile = pack(jnp.where(line <= lane, upper, lower))
    diagonal = jnp.sum(jnp.where(line == lane, lower, 0.0), axis=0, keepdims=True)
    pad = jnp.zeros((1, LANES - k), jnp.float32)
    return [tile[i : i + 1] for i in range(tile.shape[0])] + [jnp.concatenate([diagonal, pad], axis=1)]


def unpack_two(row, k):
    line, lane = places(k)
    pieces = [row[:, i : i + LANES] for i in range(0, row.shape[1], LANES)]
    square = unpack(jnp.concatenate(pieces[:-1], axis=0), k)
    turned = square.T
    upper = jnp.where(line <= lane, square, turned)
    lower = jnp.where(line > lane, square, jnp.where(line < lane, turned, jnp.broadcast_to(pieces[-1][:, :k], (k, k))))
    return upper, lower


def pair(a, b, c, d):
    over_a = 1.0 / a
    ratio = b * over_a
    over_d = 1.0 / (d - c * ratio)

    def solve(x, y):
        x = x * over_a
        y = (y - c * x) * over_d
        return x - ratio * y, y

    return solve


def solved(matrix, sides):
    k = matrix.shape[0]
    table = jnp.concatenate([matrix, sides, jnp.zeros((k, LANES - 2 * k), jnp.float32)], axis=1)
    line = lax.broadcasted_iota(jnp.int32, table.shape, 0)
    for step in range(0, k, 4):
        columns = [jnp.broadcast_to(table[:, step + i : step + i + 1], table.shape) for i in range(4)]
        rows = [table[step + i : step + i + 1] for i in range(4)]
        block = [[columns[j][step + i : step + i + 1] for j in range(4)] for i in range(4)]
        upper = pair(*block[0][:2], *block[1][:2])
        sides = [upper(block[0][j], block[1][j]) for j in (2, 3)]
        first = upper(rows[0], rows[1])
        lower = [
            [block[i][j] - (block[i][0] * sides[j - 2][0] + block[i][1] * sides[j - 2][1]) for j in (2, 3)]
            for i in (2, 3)
        ]
        rest = [rows[i] - (block[i][0] * first[0] + block[i][1] * first[1]) for i in (2, 3)]
        third, fourth = pair(*lower[0], *lower[1])(*rest)
        new = [first[i] - (sides[0][i] * third + sides[1][i] * fourth) for i in (0, 1)] + [third, fourth]
        table = table - (columns[0] * new[0] + columns[1] * new[1]) - (columns[2] * new[2] + columns[3] * new[3])
        for i in range(4):
            table = jnp.where(line == step + i, new[i], table)
    return table[:, k : 2 * k]


def odd():
    return lax.rem(lax.axis_index("sx"), 2) == 1


def marks(both):
    rows, face = both.shape
    want = lax.broadcasted_iota(jnp.int32, (face, face), 0).astype(jnp.float32)
    match = jnp.broadcast_to(both[rows - 1 : rows, :], (face, face))
    return jnp.where(want == match, 1.0, 0.0).astype(jnp.bfloat16)


def chosen_kernel(both, chosen):
    chosen[...] = marks(both)


def join_kernel(both, following, residual, rounded):
    k = residual.shape[0]
    face = both.shape[1]
    residual[:, :face] = both[:k, :]
    residual[:, face:] = select(following[:k, :], marks(following), 0)
    rounded[...] = residual[...].astype(jnp.bfloat16)


def near_kernel(size, own, beside, matrix, part, rest, held, sems):
    me = lax.axis_index("sy")
    rows, width = matrix.shape[0], own.shape[1]
    step = min(256, rows)
    copies = []
    for d in range(size):
        columns = pl.ds(pl.multiple_of((me ^ d) * width, width), width)
        target = held.at[d] if d < 2 else rest.at[d - 2]
        copies.append(pltpu.make_async_copy(matrix.at[:, columns], target, sems.at[d]))
        copies[-1].start()
    for d, block in enumerate((own, beside)):
        copies[d].wait()
        for n in range(0, rows, step):
            made = lax.dot_general(
                block[...], held[d, n : n + step, :], (((1,), (1,)), ((), ())), preferred_element_type=jnp.float32
            )
            part[:, n : n + step] = made if d == 0 else part[:, n : n + step] + made
    for d in range(2, size):
        copies[d].wait()


def far_kernel(far, mode, *refs):
    blocks = refs[:far]
    rest, part, weights, chosen = refs[far : far + 4]
    rows = part.shape[1]
    half = rows // 2
    step = min(256, half)
    if mode == "first":
        product, swap_even, swap_odd, tile = refs[far + 4 :]
    elif mode == "both":
        earlier, product, swap_even, swap_odd, out = refs[far + 4 :]
    elif mode == "one":
        product, swap_even, swap_odd, out = refs[far + 4 :]
    else:
        product, passed, out = refs[far + 4 :]
    for n in range(0, rows, step):
        made = part[:, n : n + step]
        for d in range(far):
            made = made + lax.dot_general(
                blocks[d][...], rest[d, n : n + step, :], (((1,), (1,)), ((), ())), preferred_element_type=jnp.float32
            )
        product[:, n : n + step] = made
    if mode == "last":
        passed[...] = product[:, half:]
    else:
        picked = select(product[:, :half], chosen[...], 0)
        right = product[:, half:]
        swap_even[...] = jnp.where(odd(), picked, right)
        swap_odd[...] = jnp.where(odd(), right, picked)
    fresh = gram(weights[...], product[...])
    if mode == "first":
        tile[...] = halved(fresh)
    elif mode == "both":
        for i, row in enumerate(pack_two(earlier[...], halved(fresh))):
            out[:, :, i * LANES : (i + 1) * LANES] = jnp.broadcast_to(row[None], (out.shape[0], 1, LANES))
    else:
        out[...] = jnp.broadcast_to(pack(fresh)[None], out.shape)


def assembled(product, got_even, got_odd, chosen):
    half = product.shape[1] // 2
    from_left = jnp.where(odd(), got_even[...], got_odd[...])
    from_right = jnp.where(odd(), got_odd[...], got_even[...])
    left = product[:, :half] + select(from_left, chosen[...], 1)
    return jnp.concatenate([left, product[:, half:] + from_right], axis=1)


def direction_kernel(product, got_even, got_odd, chosen, search, rounded):
    search[...] = assembled(product, got_even, got_odd, chosen)
    rounded[...] = search[...].astype(jnp.bfloat16)


def alpha_kernel(partials, alpha, gamma):
    gamma[...], delta = unpack_two(jnp.sum(partials[...], axis=0), alpha.shape[0])
    alpha[...] = solved(delta, gamma[...])


def residual_kernel(alpha, product, got_even, got_odd, chosen, residual, new_residual, rounded):
    image = assembled(product, got_even, got_odd, chosen)
    new_residual[...] = residual[...] - combine(alpha[...], image)
    rounded[...] = new_residual[...].astype(jnp.bfloat16)


def aside_kernel(gamma, alpha, search, inverse, moved):
    k, half = moved.shape
    line, lane = places(k)
    inverse[...] = solved(gamma[...], jnp.where(line == lane, 1.0, 0.0).astype(jnp.float32))
    moved[...] = combine(alpha[...], search[:, :half])


def beta_kernel(partials, inverse, beta, gnew):
    gnew[...] = halved(unpack(jnp.sum(partials[...], axis=0), gnew.shape[0]))
    beta[...] = lax.dot_general(
        inverse[...], gnew[...], (((1,), (0,)), ((), ())), precision=HIGH, preferred_element_type=jnp.float32
    )


def search_kernel(beta, product, got_even, got_odd, chosen, search, new_search, rounded):
    new_search[...] = assembled(product, got_even, got_odd, chosen) + combine(beta[...], search[...])
    rounded[...] = new_search[...].astype(jnp.bfloat16)


def last_alpha_kernel(partials, gnew, alpha):
    delta = halved(unpack(jnp.sum(partials[...], axis=0), alpha.shape[0]))
    alpha[...] = solved(delta, gnew[...])


def last_kernel(alpha, product, from_left, chosen, residual, moved, new_search, sol, res):
    half = product.shape[1] // 2
    left = product[:, :half] + select(from_left[...], chosen[...], 1)
    res[...] = residual[:, :half] - combine(alpha[...], left)
    sol[...] = moved[...] + combine(alpha[...], new_search[:, :half])


def spread(partials):
    return lax.all_to_all(partials, AXES, 0, 0)


def shards(schur, precond, right_side, matching):
    schur_rows = schur[0]
    precond_rows = precond[0]
    start = right_side[0]
    k, face = start.shape
    size = lax.axis_size("sy")
    count = lax.axis_size("sx") * size
    tile_rows = k * k // LANES
    above = lax.pad(start, jnp.float32(0), ((0, 1, 0), (0, 0, 0)))
    below = lax.pad(matching, jnp.int32(0), ((k, 0, 0), (0, 0, 0)))
    both = above + below.astype(jnp.float32)
    following = passed_along(both, -1)
    chosen = call(chosen_kernel, bf16(face, face), both)

    def apply(rounded, matrix, weights, mode, *earlier):
        far = [partner(rounded, d) for d in range(2, size)]
        beside = partner(rounded, 1)
        rows, width = matrix.shape[0], rounded.shape[1]
        room = 2 * matrix.size + (4 << 20)
        part, rest = call(
            functools.partial(near_kernel, size), (f32(k, rows), bf16(size - 2, rows, width)), rounded, beside, matrix,
            places=[VMEM, VMEM, pl.BlockSpec(memory_space=pltpu.HBM)],
            scratch=(pltpu.VMEM((2, rows, width), jnp.bfloat16), pltpu.SemaphoreType.DMA((size,))),
            room=BUDGET - matrix.size * 7 // 4,
        )
        swap = (f32(k, face), f32(k, face))
        outs = {
            "first": (f32(k, rows), *swap, f32(k, k)),
            "both": (f32(k, rows), *swap, f32(count, 1, (tile_rows + 1) * LANES)),
            "one": (f32(k, rows), *swap, f32(count, tile_rows, LANES)),
            "last": (f32(k, rows), f32(k, face), f32(count, tile_rows, LANES)),
        }[mode]
        return call(
            functools.partial(far_kernel, len(far), mode), outs, *far, rest, part, weights, chosen, *earlier, room=room
        )

    vectors = (f32(k, 2 * face), bf16(k, 2 * face))
    residual, rounded = call(join_kernel, vectors, both, following)
    product, even, odd_, tile = apply(rounded, precond_rows, residual, "first")
    got_even, got_odd = traded(odd_, even)
    search, rounded = call(direction_kernel, vectors, product, got_even, got_odd, chosen)

    product, even, odd_, partials = apply(rounded, schur_rows, search, "both", tile)
    partials = spread(partials)
    got_even, got_odd = traded(odd_, even)
    alpha, gamma = call(alpha_kernel, (f32(k, k), f32(k, k)), partials)
    residual, rounded = call(residual_kernel, vectors, alpha, product, got_even, got_odd, chosen, residual)

    inverse, moved = call(aside_kernel, (f32(k, k), f32(k, face)), gamma, alpha, search)
    product, even, odd_, partials = apply(rounded, precond_rows, residual, "one")
    partials = spread(partials)
    got_even, got_odd = traded(odd_, even)
    beta, gnew = call(beta_kernel, (f32(k, k), f32(k, k)), partials, inverse)
    new_search, rounded = call(search_kernel, vectors, beta, product, got_even, got_odd, chosen, search)

    product, passed, partials = apply(rounded, schur_rows, new_search, "last")
    partials = spread(partials)
    from_left = passed_along(passed, 1)
    alpha = call(last_alpha_kernel, f32(k, k), partials, gnew)
    sol, res = call(
        last_kernel, (f32(k, face), f32(k, face)),
        alpha, product, from_left, chosen, residual, moved, new_search,
    )
    return (sol[None], res[None])


def solution(mesh):
    in_specs = (P("sx", "sy", None), P("sx", "sy", None), P("sx", None, "sy"), P("sx", "sy"))
    out_specs = (P("sx", None, "sy"), P("sx", None, "sy"))
    return jax.shard_map(shards, mesh=mesh, in_specs=in_specs, out_specs=out_specs, check_vma=False)
```
